32 devices in a mesh: ctx: 4 (over z), node: 4 (over y, core), local: 2 (over x).
Axes of the slice: x: 2, y: 2, z: 4, core: 2. Of those that a mesh axis runs over, the one named last changes fastest.
Arguments:
- tokens: bfloat16 [1024, 3584], P(('node', 'local'), 'ctx'), may hold values from -6 to 6
- expert_ids: int32 [1024, 4], P(('node', 'local')), may hold values from 0 to 7, as said below
- route_scores: float32 [1024, 4], P(('node', 'local')), may hold values from 0.05 to 1
- w_gate: bfloat16 [8, 3584, 2048], P(('node', 'local'), None, 'ctx'), may hold values from -0.09375 to 0.09375
- w_up: bfloat16 [8, 3584, 2048], P(('node', 'local'), None, 'ctx'), may hold values from -0.09375 to 0.09375
- w_down: bfloat16 [8, 2048, 3584], P(('node', 'local'), None, 'ctx'), may hold values from -0.125 to 0.125
- shared_gate: bfloat16 [3584, 2048], P(None, 'ctx'), may hold values from -0.09375 to 0.09375
- shared_up: bfloat16 [3584, 2048], P(None, 'ctx'), may hold values from -0.09375 to 0.09375
- shared_down: bfloat16 [2048, 3584], P(None, 'ctx'), may hold values from -0.125 to 0.125
Outputs:
- mixed: bfloat16 [1024, 3584], P(('node', 'local'), 'ctx')
The draws below stay inside these ranges and needn't reach their ends.
Inputs may be any that keep to these rules, and one draw needn't show every extreme that they name: `expert_ids`: each row names 4 different experts: two in each of two different node groups, where expert e lies in group e // 2. In each aligned block of 128 rows (the rows of one index of node+local) no group is named by more than 80 rows and no expert more than 80 times; one group, the same in every block, is named by exactly 80 rows in every block, and one of its experts, the same in every block, exactly 80 times.
All inputs are finite; a program needn't handle non-finite values.
Results may differ from the reference program's by a relative error of at most 0.0064.
Values may be sent and summed in bfloat16 or wider, within the bound.
A program may use at most 64 MiB of HBM per device.

```python
import math
import jax
import jax.numpy as jnp
from jax import lax

D = 3584
FF = 2048
TOK_DEV = 128
TOPK = 4
GROUPS = 4
GROUP_EXPERTS = 2
EXPERTS = 8
GCAP = 80
SLOTS = 640
TOKENS = 1024
N_NODE = 4
N_LOCAL = 2


def draw_expert_ids(key, part):
    picks = 2 * TOK_DEV
    group_slots = GROUPS * GCAP
    blocks = N_NODE * N_LOCAL
    favored_group = jax.random.randint(jax.random.fold_in(key, 7), (), 0, GROUPS)
    favored_local = jax.random.randint(jax.random.fold_in(key, 8), (), 0, GROUP_EXPERTS)
    owners = jnp.arange(group_slots, dtype=jnp.int32) // GCAP
    group_range = jnp.arange(GROUPS, dtype=jnp.int32)
    local_range = jnp.arange(GROUP_EXPERTS, dtype=jnp.int32)

    def one_block(block_key):
        first_key, second_key, third_key, fourth_key = jax.random.split(block_key, 4)
        priority = jax.random.permutation(first_key, group_slots).astype(jnp.int32)
        priority = jnp.where(owners == favored_group, priority - group_slots, priority)
        ordering = jnp.argsort(priority, stable=True)
        chosen = jnp.sort(ordering[:picks])
        group_list = (chosen // GCAP).astype(jnp.int32)
        table = group_list.reshape(2, TOK_DEV).T
        table = table[jax.random.permutation(second_key, TOK_DEV)]
        joined = jnp.any(table[:, :, None] == group_range[None, None, :], axis=1).astype(jnp.int32)
        group_rank = jnp.cumsum(joined, axis=0) - joined
        rank_pick = jnp.take_along_axis(group_rank, table, axis=1)
        perm_keys = jax.random.split(third_key, GROUPS)
        perms = jax.vmap(lambda one_key: jax.random.permutation(one_key, GROUP_EXPERTS))(perm_keys).astype(jnp.int32)
        position = jnp.argsort(perms, axis=1).astype(jnp.int32)
        forced = (group_range[:, None] == favored_group) & (local_range[None, :] == favored_local)
        position = jnp.where(forced, -1, position)
        perm_table = jnp.argsort(position, axis=1, stable=True).astype(jnp.int32)
        first_pos = 2 * rank_pick % GROUP_EXPERTS
        second_pos = (2 * rank_pick + 1) % GROUP_EXPERTS
        first_local = perm_table[table, first_pos]
        second_local = perm_table[table, second_pos]
        first_ids = table * GROUP_EXPERTS + first_local
        second_ids = table * GROUP_EXPERTS + second_local
        ids = jnp.stack([first_ids[:, 0], second_ids[:, 0], first_ids[:, 1], second_ids[:, 1]], axis=1)
        scores = jax.random.randint(fourth_key, (TOK_DEV, TOPK), 0, 1 << 20) * TOPK + jnp.arange(TOPK, dtype=jnp.int32)[None, :]
        order = jnp.argsort(scores, axis=1)
        return jnp.take_along_axis(ids, order, axis=1).astype(jnp.int32)
    block_keys = jax.random.split(jax.random.fold_in(key, 11), blocks)
    result = jax.vmap(one_block)(block_keys)
    return result.reshape(blocks * TOK_DEV, TOPK).astype(jnp.int32)


def block_levels(stream_key, extent, cuts, smallest, largest):
    def one(dim, blocks):
        steps = jax.random.uniform(jax.random.fold_in(jax.random.fold_in(stream_key, 6), dim), (blocks,), jnp.float32, smallest / len(cuts), largest / len(cuts))
        return jnp.repeat(jnp.exp(steps), extent[dim] // blocks).reshape((-1,) + (1,) * (len(extent) - dim - 1))

    level = one(*cuts[0])
    for cut in cuts[1:]:
        level = level * one(*cut)
    return level


def bell_draw(key, shape, width, most, pieces=(), held_as=jnp.bfloat16):
    entries = jax.random.normal(key, shape, jnp.float32) * width
    if len(pieces) > 0:
        entries = block_levels(key, shape, pieces, -0.22, 0.18) * entries
    return jnp.clip(entries, min=-most, max=most).astype(held_as)


def setup_inputs(seed: int = 0) -> dict:
    key_list = jax.random.split(jax.random.key(seed), 10)
    return {
        "tokens": bell_draw(key_list[0], (TOKENS, D), 1.0, 6.0, ((0, 8), (1, 4))),
        "expert_ids": draw_expert_ids(jax.random.fold_in(key_list[9], 71), 0),
        "route_scores": jnp.clip(jnp.exp(math.log(1.0) - 2.9957323 * jax.random.uniform(key_list[2], (TOKENS, TOPK), jnp.float32) ** block_levels(key_list[2], (TOKENS, TOPK), ((0, 8),), -0.2, 0.2)), 0.05, 1.0),
        "w_gate": bell_draw(key_list[3], (EXPERTS, D, FF), D ** -0.5, 0.09375, ((0, 8), (2, 4))),
        "w_up": bell_draw(key_list[4], (EXPERTS, D, FF), D ** -0.5, 0.09375, ((0, 8), (2, 4))),
        "w_down": bell_draw(key_list[5], (EXPERTS, FF, D), FF ** -0.5, 0.125, ((0, 8), (2, 4))),
        "shared_gate": bell_draw(key_list[6], (D, FF), D ** -0.5, 0.09375, ((1, 4),)),
        "shared_up": bell_draw(key_list[7], (D, FF), D ** -0.5, 0.09375, ((1, 4),)),
        "shared_down": bell_draw(key_list[8], (FF, D), FF ** -0.5, 0.125, ((1, 4),)),
    }


route_scale = 2.5


def expert_pass(inputs, gate_matrix, up_matrix, down_matrix):
    gate_value = jnp.dot(inputs, gate_matrix, preferred_element_type=jnp.float32)
    up_value = jnp.dot(inputs, up_matrix, preferred_element_type=jnp.float32)
    hidden = (jax.nn.silu(gate_value) * up_value).astype(jnp.bfloat16)
    return jnp.dot(hidden, down_matrix, preferred_element_type=jnp.float32)


def reference(tokens, expert_ids, route_scores, w_gate, w_up, w_down, shared_gate, shared_up, shared_down):
    scaled = route_scale * route_scores / jnp.sum(route_scores, axis=1, keepdims=True)
    gate_weights = lax.optimization_barrier(scaled.astype(jnp.bfloat16)).astype(jnp.float32)
    shared_out = expert_pass(tokens, shared_gate, shared_up, shared_down)

    def one_expert(index):
        chosen = expert_ids == index
        member = jnp.any(chosen, axis=1)
        weight_column = jnp.sum(jnp.where(chosen, gate_weights, 0.0), axis=1)
        positions = jnp.nonzero(member, size=SLOTS, fill_value=0)[0].astype(jnp.int32)
        valid = jnp.arange(SLOTS, dtype=jnp.int32) < jnp.sum(member.astype(jnp.int32))
        outputs = expert_pass(tokens[positions], w_gate[index], w_up[index], w_down[index]).astype(jnp.bfloat16)
        outputs = lax.optimization_barrier(outputs).astype(jnp.float32)
        scale_column = jnp.where(valid, weight_column[positions], 0.0)
        return positions, outputs * scale_column[:, None]

    positions, contribs = lax.map(one_expert, jnp.arange(EXPERTS, dtype=jnp.int32))
    positions = positions.reshape(GROUPS, GROUP_EXPERTS * SLOTS)
    contribs = contribs.reshape(GROUPS, GROUP_EXPERTS * SLOTS, D)

    def add_group(group, total):
        routed = jnp.zeros((TOKENS, D), jnp.float32).at[positions[group]].add(contribs[group])
        rounded = lax.optimization_barrier(routed.astype(jnp.bfloat16)).astype(jnp.float32)
        return total + rounded

    mixed = lax.fori_loop(0, GROUPS, add_group, shared_out.astype(jnp.float32))
    return mixed.astype(jnp.bfloat16)
```

```python
import jax
import jax.numpy as jnp
from jax import lax
from jax.experimental import pallas as pl
from jax.experimental.pallas import tpu as pltpu
from jax.sharding import PartitionSpec as P

route_scale = 2.5
MESH = pl.DeviceIdType.MESH
VMEM_BYTES = 64000 * 1024


def matmul(left_side, right_side):
    return jnp.dot(left_side, right_side, preferred_element_type=jnp.float32)


def exchange(
    tokens, expert_ids, route_scores, w_gate, w_up, w_down, shared_gate, shared_up, shared_down
):
    tok_count = tokens.shape[0]
    feat_local = tokens.shape[1]
    top_count = expert_ids.shape[1]
    group_count = lax.axis_size("node")
    member_count = lax.axis_size("local")
    expert_count = group_count * member_count
    group_cap = (10 * tok_count + 4 * group_count - 1) // (4 * group_count)
    capacity = (2 * group_cap + member_count - 1) // member_count
    slot_total = expert_count * capacity
    gate_local = w_gate[0]
    up_local = w_up[0]
    down_local = w_down[0]
    out_width = down_local.shape[1]
    scaled = route_scale * route_scores / jnp.sum(route_scores, axis=1, keepdims=True)
    gate_weights = lax.optimization_barrier(scaled.astype(jnp.bfloat16)).astype(jnp.float32)
    group_range = jnp.arange(group_count, dtype=jnp.int32)
    group_onehot = (expert_ids // member_count)[:, :, None] == group_range[None, None, :]
    flat_ids = expert_ids.reshape(-1)
    pair_count = flat_ids.shape[0]
    onehot = (flat_ids[:, None] == jnp.arange(expert_count, dtype=jnp.int32)[None, :]).astype(
        jnp.int32
    )
    earlier = jnp.cumsum(onehot, axis=0) - onehot
    ranking = jnp.sum(earlier * onehot, axis=1)
    pair_slot = flat_ids * capacity + ranking
    pair_token = jnp.arange(pair_count, dtype=jnp.int32) // top_count
    matches = pair_slot[None, :] == jnp.arange(slot_total, dtype=jnp.int32)[:, None]
    slot_token = jnp.where(
        jnp.any(matches, axis=1),
        jnp.sum(jnp.where(matches, pair_token[None, :], 0), axis=1),
        tok_count,
    )
    padded_tokens = jnp.concatenate([tokens, jnp.zeros((1, feat_local), tokens.dtype)], axis=0)
    send_rows = padded_tokens[slot_token].reshape(group_count, member_count, capacity * feat_local)
    arrived = lax.all_to_all(
        lax.all_to_all(send_rows, "node", split_axis=0, concat_axis=0, tiled=True),
        "local",
        split_axis=1,
        concat_axis=1,
        tiled=True,
    )
    routed_rows = arrived.reshape(slot_total, feat_local)
    stacked = jnp.concatenate([routed_rows, tokens], axis=0)
    segment = lax.all_gather(stacked, "ctx", axis=1, tiled=True)
    routed_part = segment[:slot_total]
    shared_part = segment[slot_total:]
    gate_routed = matmul(routed_part, gate_local)
    up_routed = matmul(routed_part, up_local)
    gate_shared = matmul(shared_part, shared_gate)
    up_shared = matmul(shared_part, shared_up)
    routed_hidden = (jax.nn.silu(gate_routed) * up_routed).astype(jnp.bfloat16)
    shared_hidden = (jax.nn.silu(gate_shared) * up_shared).astype(jnp.bfloat16)
    hidden_stack = jnp.concatenate([routed_hidden, shared_hidden], axis=0)
    segment = lax.all_gather(hidden_stack, "ctx", axis=1, tiled=True)
    routed_out = matmul(segment[:slot_total], down_local)
    shared_out = matmul(segment[slot_total:], shared_down)
    routed_bf = routed_out.astype(jnp.bfloat16)
    sendback = routed_bf.reshape(group_count, member_count, capacity * out_width)
    returned = lax.all_to_all(
        lax.all_to_all(sendback, "node", split_axis=0, concat_axis=0, tiled=True),
        "local",
        split_axis=1,
        concat_axis=1,
        tiled=True,
    )
    returned = returned.reshape(slot_total, out_width)
    pair_out = returned[pair_slot].reshape(tok_count, top_count, out_width).astype(jnp.float32)
    weighted = gate_weights[:, :, None] * pair_out
    group_sum = jnp.einsum(
        "tkg,tkd->tgd", group_onehot.astype(jnp.float32), weighted, precision=lax.Precision.HIGHEST
    )
    rounded = lax.optimization_barrier(group_sum.astype(jnp.bfloat16)).astype(jnp.float32)
    routed_sum = jnp.sum(rounded, axis=1)
    mixed = shared_out + routed_sum
    return mixed.astype(jnp.bfloat16)


def column_tiles(width, tile, visit):
    whole = width // tile
    if whole == 1:
        visit(0, tile)
    elif whole > 1:

        def step(index, carry):
            visit(pl.multiple_of(index * tile, tile), tile)
            return carry

        lax.fori_loop(0, whole, step, 0)
    if width % tile:
        visit(whole * tile, width % tile)


def cube_kernel(
    sizes,
    tok_in,
    ids_in,
    scores_in,
    wg_in,
    wu_in,
    wd_in,
    sg_in,
    su_in,
    sd_in,
    out_ref,
    tok,
    meta,
    wg,
    wu,
    wd,
    sg,
    su,
    sd,
    rows_in,
    hid_s,
    hid,
    part,
    got,
    total,
    sum_g,
    sum_u,
    acc_g,
    acc_u,
    hold,
    loc_sem,
    z_send,
    z_recv,
    b_send,
    b_recv,
    m_send,
    m_recv,
    p_send,
    p_recv,
):
    ctx_count, group_count, member_count, cap = sizes
    c = lax.axis_index("ctx")
    n = lax.axis_index("node")
    l = lax.axis_index("local")
    last = ctx_count - 1
    tok_count = tok.shape[2]
    feat = tok.shape[3]
    width = wg.shape[1]
    out_width = wd.shape[1]
    slots = range(1, tok.shape[0])

    def peer(slot):
        node = n
        if slot & 1:
            node = node + 1 - 2 * lax.rem(node, 2)
        if slot & 4:
            node = lax.rem(node + group_count // 2, group_count)
        member = lax.rem(l + 1, member_count) if slot & 2 else l
        return {"node": node, "local": member}

    first = pltpu.make_async_copy(tok_in, tok.at[0, c], loc_sem.at[0])
    first.start()
    loads = []
    for index, (src, dst) in enumerate(
        ((sg_in, sg), (su_in, su), (wg_in, wg), (wu_in, wu), (sd_in, sd), (wd_in, wd))
    ):
        loads.append(pltpu.make_async_copy(src, dst, loc_sem.at[2 + index]))

    barrier = pltpu.get_barrier_semaphore()
    for slot in slots:
        pl.semaphore_signal(barrier, inc=1, device_id=peer(slot), device_id_type=MESH)

    @pl.when(c > 0)
    def _():
        pl.semaphore_signal(barrier, inc=1, device_id={"ctx": c - 1}, device_id_type=MESH)

    @pl.when(c < last)
    def _():
        pl.semaphore_signal(barrier, inc=1, device_id={"ctx": c + 1}, device_id_type=MESH)

    for load in loads:
        load.start()

    inner = (c > 0) & (c < last)

    @pl.when(inner)
    def _():
        pl.semaphore_wait(barrier, len(slots) + 2)

    @pl.when(jnp.logical_not(inner))
    def _():
        pl.semaphore_wait(barrier, len(slots) + 1)

    first.wait()

    SHARED = 2
    PAIR = 3
    half_rows = tok_count // 2

    def piece(chunk, shard):
        if chunk < 2:
            return tok.at[0, shard, pl.ds(chunk * half_rows, half_rows)]
        if chunk == SHARED:
            return hid_s.at[shard]
        return hid.at[chunk - PAIR, shard]

    def line(chunk, depth, way, shard, target):
        return pltpu.make_async_remote_copy(
            src_ref=piece(chunk, shard),
            dst_ref=piece(chunk, shard),
            send_sem=z_send.at[way, depth, chunk],
            recv_sem=z_recv.at[way, depth, chunk],
            device_id={"ctx": target},
            device_id_type=MESH,
        )

    def line_send(chunk, depth, finish=False):
        for way in (0, 1):
            shard, target = (c - depth, c + 1) if way == 0 else (c + depth, c - 1)
            ready = (c >= depth) & (c < last) if way == 0 else (c + depth <= last) & (c > 0)

            @pl.when(ready)
            def _():
                copy = line(chunk, depth, way, shard, target)
                if finish:
                    copy.wait_send()
                else:
                    copy.start()

    def line_take(chunk, depth, relays, then=None):
        for way in (0, 1):
            shard = c - 1 - depth if way == 0 else c + 1 + depth
            source = c - 1 if way == 0 else c + 1
            target = c + 1 if way == 0 else c - 1
            here = shard >= 0 if way == 0 else shard <= last
            passes = target < ctx_count if way == 0 else target >= 0
            if depth == last - 1:
                if relays:
                    continue
            else:
                here = here & (passes if relays else jnp.logical_not(passes))

            @pl.when(here)
            def _():
                line(chunk, depth, way, shard, source).wait_recv()
                if relays:
                    line(chunk, depth + 1, way, shard, target).start()
                if then is not None:
                    then(shard)

    def relay_line(chunk, depth, then=None):
        line_take(chunk, depth, True, then)

    def await_line(chunk):
        for depth in range(last):
            line_take(chunk, depth, False)

    def at_stage(stage, then):
        if stage == 0:
            then(c)
            return
        for shard in (c - stage, c + stage):

            @pl.when((shard >= 0) & (shard <= last))
            def _():
                then(shard)

    def hand(src_slot, dst_slot, shard, over):
        return pltpu.make_async_remote_copy(
            src_ref=tok.at[src_slot, shard],
            dst_ref=tok.at[dst_slot, shard],
            send_sem=b_send.at[dst_slot, shard],
            recv_sem=b_recv.at[dst_slot, shard],
            device_id=peer(over),
            device_id_type=MESH,
        )

    def spread(shard):
        hand(0, 1, shard, 1).start()
        hand(0, 2, shard, 2).start()
        hand(0, 4, shard, 4).start()

    def take(slot, shard):
        hand(0, slot, shard, 1).wait_recv()

    line_send(0, 0)
    line_send(1, 0)

    scores = scores_in[...]
    scaled = route_scale * scores / jnp.sum(scores, axis=0, keepdims=True)
    gates = scaled.astype(jnp.bfloat16).astype(jnp.float32)
    row = lax.broadcasted_iota(jnp.int32, meta.shape[1:], 0)
    named = jnp.zeros(row.shape, jnp.float32)
    table = jnp.zeros(row.shape, jnp.float32)
    for k in range(ids_in.shape[0]):
        expert = ids_in[k : k + 1, :]
        named = jnp.where(row == expert // member_count, 1.0, named)
        table = table + jnp.where(row == expert + group_count, gates[k : k + 1, :], 0.0)
    square = (tok_count, tok_count)
    before = lax.broadcasted_iota(jnp.int32, square, 0) < lax.broadcasted_iota(jnp.int32, square, 1)
    counts = matmul(named.astype(jnp.bfloat16), jnp.where(before, 1.0, 0.0).astype(jnp.bfloat16))
    meta[0] = jnp.where(row < group_count, jnp.where(named > 0.5, counts, -1.0), table)

    greet = []
    for slot in slots:
        greet.append(
            pltpu.make_async_remote_copy(
                src_ref=meta.at[0],
                dst_ref=meta.at[slot],
                send_sem=m_send.at[slot],
                recv_sem=m_recv.at[slot],
                device_id=peer(slot),
                device_id_type=MESH,
            )
        )
        greet[-1].start()
    spread(c)

    def columns(shard):
        return pl.ds(pl.multiple_of(shard * feat, 128), feat)

    def shared_add(shard, fresh=False):
        ins = columns(shard)

        def visit(start, size):
            cols = pl.ds(start, size)
            g = matmul(tok[0, shard], sg[ins, cols])
            u = matmul(tok[0, shard], su[ins, cols])
            sum_g[:, cols] = g if fresh else sum_g[:, cols] + g
            sum_u[:, cols] = u if fresh else sum_u[:, cols] + u

        column_tiles(width, 256, visit)

    rank_of = lambda slot: meta[slot, pl.ds(n, 1), :]
    weight_of = lambda slot: meta[slot, pl.ds(group_count + n * member_count + l, 1), :]

    def mask_of(slot):
        spots = lax.broadcasted_iota(jnp.int32, (cap, tok_count), 0).astype(jnp.float32)
        return jnp.where(spots == rank_of(slot), 1.0, 0.0).astype(jnp.bfloat16)

    def pair_add(shard, fresh=False):
        ins = columns(shard)
        for place, slot in enumerate(pairs[3]):
            chosen = matmul(mask_of(slot), tok[slot, shard]).astype(jnp.bfloat16)
            rows_in[place * cap : (place + 1) * cap, ins] = chosen

        def visit(start, size):
            cols = pl.ds(start, size)
            g = matmul(rows_in[0 : 2 * cap, ins], wg[ins, cols])
            u = matmul(rows_in[0 : 2 * cap, ins], wu[ins, cols])
            acc_g[:, cols] = g if fresh else acc_g[:, cols] + g
            acc_u[:, cols] = u if fresh else acc_u[:, cols] + u

        column_tiles(width, 256, visit)

    def pick(row, slot):
        mask = mask_of(slot)

        def step(shard, carry):
            chosen = matmul(mask, tok[slot, shard]).astype(jnp.bfloat16)
            rows_in[row : row + cap, columns(shard)] = chosen
            return carry

        lax.fori_loop(0, ctx_count, step, 0)

    def hidden(count, gate, up, target):
        def visit(start, size):
            cols = pl.ds(start, size)
            g = matmul(rows_in[0:count, :], gate[:, cols])
            u = matmul(rows_in[0:count, :], up[:, cols])
            target[:, cols] = (g / (1.0 + jnp.exp(-g)) * u).astype(jnp.bfloat16)

        column_tiles(width, 256, visit)

    pairs = ((2, 3), (4, 5), (6, 7), (0, 1))

    def compute(index):
        for place, slot in enumerate(pairs[index]):
            pick(place * cap, slot)
        hidden(2 * cap, wg, wu, hid.at[index, c])

    half = ctx_count // 2

    loads[0].wait()
    loads[1].wait()
    shared_add(c, True)
    greet[0].wait_recv()
    loads[2].wait()
    loads[3].wait()
    take(1, c)
    pair_add(c, True)

    def both_add(shard):
        shared_add(shard)
        take(1, shard)
        pair_add(shard)

    for depth in range(last):
        for chunk, then in ((0, None), (1, spread)):
            for relays in (True, False):
                line_take(chunk, depth, relays, then)
        at_stage(depth + 1, both_add)

    g = acc_g[...]
    hid[3, c] = (g / (1.0 + jnp.exp(-g)) * acc_u[...]).astype(jnp.bfloat16)
    line_send(PAIR + 3, 0)
    g = sum_g[...]
    hid_s[c] = (g / (1.0 + jnp.exp(-g)) * sum_u[...]).astype(jnp.bfloat16)
    line_send(SHARED, 0)

    def relay(shard):
        take(2, shard)
        hand(2, 3, shard, 1).start()

        @pl.when(shard < half)
        def _():
            hand(2, 6, shard, 4).start()

        take(4, shard)
        hand(4, 5, shard, 1).start()

        @pl.when(shard >= half)
        def _():
            hand(4, 6, shard, 2).start()

    at_stage(0, relay)
    at_stage(1, relay)
    relay_line(PAIR + 3, 0)
    for stage in range(2, ctx_count):
        at_stage(stage, relay)
    for copy in greet[1:]:
        copy.wait_recv()
    for shard in range(ctx_count):
        take(3, shard)
    compute(0)
    line_send(PAIR, 0)
    for shard in range(ctx_count):
        take(5, shard)
    compute(1)
    line_send(PAIR + 1, 0)
    relay_line(PAIR + 3, 1)
    for shard in range(ctx_count):
        take(6, shard)
        hand(6, 7, shard, 1).start()
    relay_line(PAIR, 0)
    relay_line(PAIR + 1, 0)
    for shard in range(ctx_count):
        take(7, shard)
    compute(2)
    line_send(PAIR + 2, 0)
    relay_line(PAIR, 1)

    loads[4].wait()
    loads[5].wait()

    def product(index, down, cols):
        value = matmul(hid[index, 0], down[0:width, cols])
        for shard in range(1, ctx_count):
            value = value + matmul(
                hid[index, shard], down[shard * width : (shard + 1) * width, cols]
            )
        return value

    def shared_out(shard, fresh=False):
        units = pl.ds(pl.multiple_of(shard * width, 128), width)

        def visit(start, size):
            cols = pl.ds(start, size)
            value = matmul(hid_s[shard], sd[units, cols])
            total[:, cols] = value if fresh else total[:, cols] + value

        column_tiles(out_width, 256, visit)

    split = -(-out_width // 256) * 128
    parts = ((0, split), (split, out_width - split))
    sends = {}

    def ship(slot, over, part_index):
        cols = pl.ds(*parts[part_index])
        copy = pltpu.make_async_remote_copy(
            src_ref=part.at[slot - 1, :, cols],
            dst_ref=got.at[slot - 1, :, cols],
            send_sem=p_send.at[slot, part_index],
            recv_sem=p_recv.at[slot, part_index],
            device_id=peer(over),
            device_id_type=MESH,
        )
        sends[slot, part_index] = copy
        copy.start()

    def tiles(part_index, visit):
        begin, size = parts[part_index]
        column_tiles(size, 256, lambda start, count: visit(begin + start, count))

    def finish(index):
        weights = []
        for slot in pairs[index]:
            spots = lax.broadcasted_iota(jnp.int32, (tok_count, tok_count), 0).astype(jnp.float32)
            mask = jnp.where(spots == rank_of(slot), weight_of(slot), 0.0)
            weights.append(jnp.transpose(mask)[:, 0:cap].astype(jnp.bfloat16))

        def visit(start, size):
            cols = pl.ds(start if isinstance(start, int) else pl.multiple_of(start, 128), size)
            rows = product(index, wd, cols).astype(jnp.bfloat16)
            for place, slot in enumerate(pairs[index]):
                value = matmul(weights[place], rows[place * cap : (place + 1) * cap])
                if slot == 0:
                    total[:, cols] += value
                elif place == 0:
                    hold[:, cols] = value
                else:
                    part[slot - 1, :, cols] = value.astype(jnp.bfloat16)

        for part_index in range(2):
            tiles(part_index, visit)
            ship(pairs[index][1], 1, part_index)

    def forward(index):
        slot, other = pairs[index]

        def visit(start, size):
            cols = pl.ds(start if isinstance(start, int) else pl.multiple_of(start, 128), size)
            value = hold[:, cols] + got[other - 1, :, cols].astype(jnp.float32)
            part[slot - 1, :, cols] = value.astype(jnp.bfloat16)

        for part_index in range(2):
            sends[other, part_index].wait_recv()
            tiles(part_index, visit)
            ship(slot, slot, part_index)

    shared_out(c, True)
    await_line(PAIR + 3)
    finish(3)
    relay_line(PAIR + 1, 1)
    relay_line(PAIR + 2, 0)
    relay_line(PAIR + 2, 1)
    relay_line(SHARED, 0)
    relay_line(SHARED, 1)
    await_line(PAIR)
    finish(0)
    forward(0)
    await_line(PAIR + 1)
    finish(1)
    forward(1)
    await_line(PAIR + 2)
    finish(2)
    forward(2)

    def gather_some(start, size):
        cols = pl.ds(start, size)
        value = total[:, cols]
        for slot in (1, 2, 4):
            value = value + got[slot - 1, :, cols].astype(jnp.float32)
        total[:, cols] = value

    for slot in (1, 2, 4):
        for part_index in range(2):
            sends[slot, part_index].wait_recv()
    column_tiles(out_width, 256, gather_some)
    await_line(SHARED)
    for depth in range(last):
        at_stage(depth + 1, shared_out)

    def gather_rest(start, size):
        cols = pl.ds(start if isinstance(start, int) else pl.multiple_of(start, 128), size)
        value = total[:, cols] + got[5, :, cols].astype(jnp.float32)
        out_ref[:, cols] = value.astype(jnp.bfloat16)

    for part_index in range(2):
        sends[6, part_index].wait_recv()
        tiles(part_index, gather_rest)

    for copy in list(sends.values()) + greet:
        copy.wait_send()
    for chunk in range(PAIR + 4):
        for depth in range(last):
            line_send(chunk, depth, finish=True)
    for shard in range(ctx_count):
        for slot in (1, 2, 3, 4, 5, 6, 7):
            hand(0, slot, shard, 1).wait_send()


def cube(
    tokens, expert_ids, route_scores, w_gate, w_up, w_down, shared_gate, shared_up, shared_down
):
    ctx_count = lax.axis_size("ctx")
    group_count = lax.axis_size("node")
    member_count = lax.axis_size("local")
    expert_count = group_count * member_count
    tok_count, feat = tokens.shape
    cap = (10 * tok_count + 4 * group_count - 1) // (4 * group_count)
    hidden_units, out_width = w_down.shape[1:]
    width = w_gate.shape[2]
    meta_rows = -(-(group_count + expert_count) // 16) * 16
    slots = 2 * group_count
    bf16 = jnp.bfloat16
    rows = max(2 * cap, tok_count)
    anywhere = pl.BlockSpec(memory_space=pl.ANY)
    inside = pl.BlockSpec(memory_space=pltpu.VMEM)
    dma = pltpu.SemaphoreType.DMA
    kernel = lambda *refs: cube_kernel((ctx_count, group_count, member_count, cap), *refs)
    return pl.pallas_call(
        kernel,
        out_shape=jax.ShapeDtypeStruct((tok_count, out_width), bf16),
        in_specs=[anywhere, inside, inside] + [anywhere] * 6,
        out_specs=inside,
        scratch_shapes=[
            pltpu.VMEM((slots, ctx_count, tok_count, feat), bf16),
            pltpu.VMEM((slots, meta_rows, tok_count), jnp.float32),
            pltpu.VMEM(w_gate.shape[1:], bf16),
            pltpu.VMEM(w_up.shape[1:], bf16),
            pltpu.VMEM(w_down.shape[1:], bf16),
            pltpu.VMEM(shared_gate.shape, bf16),
            pltpu.VMEM(shared_up.shape, bf16),
            pltpu.VMEM(shared_down.shape, bf16),
            pltpu.VMEM((rows, ctx_count * feat), bf16),
            pltpu.VMEM((ctx_count, tok_count, width), bf16),
            pltpu.VMEM((4, ctx_count, 2 * cap, width), bf16),
            pltpu.VMEM((slots - 1, tok_count, out_width), bf16),
            pltpu.VMEM((slots - 1, tok_count, out_width), bf16),
            pltpu.VMEM((tok_count, out_width), jnp.float32),
            pltpu.VMEM((tok_count, width), jnp.float32),
            pltpu.VMEM((tok_count, width), jnp.float32),
            pltpu.VMEM((2 * cap, width), jnp.float32),
            pltpu.VMEM((2 * cap, width), jnp.float32),
            pltpu.VMEM((tok_count, out_width), jnp.float32),
            dma((8,)),
            dma((2, ctx_count - 1, 7)),
            dma((2, ctx_count - 1, 7)),
            dma((slots, ctx_count)),
            dma((slots, ctx_count)),
            dma((slots,)),
            dma((slots,)),
            dma((slots, 2)),
            dma((slots, 2)),
        ],
        compiler_params=pltpu.CompilerParams(
            collective_id=0, has_side_effects=True, vmem_limit_bytes=VMEM_BYTES
        ),
    )(
        tokens,
        expert_ids.T,
        route_scores.T,
        w_gate[0],
        w_up[0],
        w_down[0],
        shared_gate,
        shared_up,
        shared_down,
    )


def local(tokens, expert_ids, *rest):
    whole_groups = expert_ids.shape[1] == 2 * lax.axis_size("local")
    if whole_groups and lax.axis_size("local") == 2 and lax.axis_size("node") == 4:
        return cube(tokens, expert_ids, *rest)
    return exchange(tokens, expert_ids, *rest)


def solution(mesh):
    return jax.shard_map(
        local,
        mesh=mesh,
        in_specs=(
            P(("node", "local"), "ctx"),
            P(("node", "local"), None),
            P(("node", "local"), None),
            P(("node", "local"), None, "ctx"),
            P(("node", "local"), None, "ctx"),
            P(("node", "local"), None, "ctx"),
            P(None, "ctx"),
            P(None, "ctx"),
            P(None, "ctx"),
        ),
        out_specs=P(("node", "local"), "ctx"),
        check_vma=False,
    )
```

```python
import jax
import jax.numpy as jnp
from jax import lax
from jax.experimental import pallas as pl
from jax.experimental.pallas import tpu as pltpu
from jax.sharding import PartitionSpec as P

route_scale = 2.5
MESH = pl.DeviceIdType.MESH
VMEM_BYTES = 64000 * 1024


def matmul(left_side, right_side):
    return jnp.dot(left_side, right_side, preferred_element_type=jnp.float32)


def exchange(
    tokens, expert_ids, route_scores, w_gate, w_up, w_down, shared_gate, shared_up, shared_down
):
    tok_count = tokens.shape[0]
    feat_local = tokens.shape[1]
    top_count = expert_ids.shape[1]
    group_count = lax.axis_size("node")
    member_count = lax.axis_size("local")
    expert_count = group_count * member_count
    group_cap = (10 * tok_count + 4 * group_count - 1) // (4 * group_count)
    capacity = (2 * group_cap + member_count - 1) // member_count
    slot_total = expert_count * capacity
    gate_local = w_gate[0]
    up_local = w_up[0]
    down_local = w_down[0]
    out_width = down_local.shape[1]
    scaled = route_scale * route_scores / jnp.sum(route_scores, axis=1, keepdims=True)
    gate_weights = lax.optimization_barrier(scaled.astype(jnp.bfloat16)).astype(jnp.float32)
    group_range = jnp.arange(group_count, dtype=jnp.int32)
    group_onehot = (expert_ids // member_count)[:, :, None] == group_range[None, None, :]
    flat_ids = expert_ids.reshape(-1)
    pair_count = flat_ids.shape[0]
    onehot = (flat_ids[:, None] == jnp.arange(expert_count, dtype=jnp.int32)[None, :]).astype(
        jnp.int32
    )
    earlier = jnp.cumsum(onehot, axis=0) - onehot
    ranking = jnp.sum(earlier * onehot, axis=1)
    pair_slot = flat_ids * capacity + ranking
    pair_token = jnp.arange(pair_count, dtype=jnp.int32) // top_count
    matches = pair_slot[None, :] == jnp.arange(slot_total, dtype=jnp.int32)[:, None]
    slot_token = jnp.where(
        jnp.any(matches, axis=1),
        jnp.sum(jnp.where(matches, pair_token[None, :], 0), axis=1),
        tok_count,
    )
    padded_tokens = jnp.concatenate([tokens, jnp.zeros((1, feat_local), tokens.dtype)], axis=0)
    send_rows = padded_tokens[slot_token].reshape(group_count, member_count, capacity * feat_local)
    arrived = lax.all_to_all(
        lax.all_to_all(send_rows, "node", split_axis=0, concat_axis=0, tiled=True),
        "local",
        split_axis=1,
        concat_axis=1,
        tiled=True,
    )
    routed_rows = arrived.reshape(slot_total, feat_local)
    stacked = jnp.concatenate([routed_rows, tokens], axis=0)
    segment = lax.all_gather(stacked, "ctx", axis=1, tiled=True)
    routed_part = segment[:slot_total]
    shared_part = segment[slot_total:]
    gate_routed = matmul(routed_part, gate_local)
    up_routed = matmul(routed_part, up_local)
    gate_shared = matmul(shared_part, shared_gate)
    up_shared = matmul(shared_part, shared_up)
    routed_hidden = (jax.nn.silu(gate_routed) * up_routed).astype(jnp.bfloat16)
    shared_hidden = (jax.nn.silu(gate_shared) * up_shared).astype(jnp.bfloat16)
    hidden_stack = jnp.concatenate([routed_hidden, shared_hidden], axis=0)
    segment = lax.all_gather(hidden_stack, "ctx", axis=1, tiled=True)
    routed_out = matmul(segment[:slot_total], down_local)
    shared_out = matmul(segment[slot_total:], shared_down)
    routed_bf = routed_out.astype(jnp.bfloat16)
    sendback = routed_bf.reshape(group_count, member_count, capacity * out_width)
    returned = lax.all_to_all(
        lax.all_to_all(sendback, "node", split_axis=0, concat_axis=0, tiled=True),
        "local",
        split_axis=1,
        concat_axis=1,
        tiled=True,
    )
    returned = returned.reshape(slot_total, out_width)
    pair_out = returned[pair_slot].reshape(tok_count, top_count, out_width).astype(jnp.float32)
    weighted = gate_weights[:, :, None] * pair_out
    group_sum = jnp.einsum(
        "tkg,tkd->tgd", group_onehot.astype(jnp.float32), weighted, precision=lax.Precision.HIGHEST
    )
    rounded = lax.optimization_barrier(group_sum.astype(jnp.bfloat16)).astype(jnp.float32)
    routed_sum = jnp.sum(rounded, axis=1)
    mixed = shared_out + routed_sum
    return mixed.astype(jnp.bfloat16)


def column_tiles(width, tile, visit):
    whole = width // tile
    if whole == 1:
        visit(0, tile)
    elif whole > 1:

        def step(index, carry):
            visit(pl.multiple_of(index * tile, tile), tile)
            return carry

        lax.fori_loop(0, whole, step, 0)
    if width % tile:
        visit(whole * tile, width % tile)


def cube_kernel(
    sizes,
    tok_in,
    ids_in,
    scores_in,
    wg_in,
    wu_in,
    wd_in,
    sg_in,
    su_in,
    sd_in,
    out_ref,
    tok,
    meta,
    wg,
    wu,
    wd,
    sg,
    su,
    sd,
    rows_in,
    hid_s,
    hid,
    part,
    got,
    total,
    sum_g,
    sum_u,
    acc_g,
    acc_u,
    hold,
    blend,
    rows_out,
    near_wd,
    near_part,
    near_got,
    near_hold,
    near_sum,
    end_sum,
    loc_sem,
    z_send,
    z_recv,
    b_send,
    b_recv,
    m_send,
    m_recv,
    p_send,
    p_recv,
    w_send,
    w_recv,
    x_send,
    x_recv,
):
    ctx_count, group_count, member_count, cap = sizes
    c = lax.axis_index("ctx")
    n = lax.axis_index("node")
    l = lax.axis_index("local")
    last = ctx_count - 1
    tok_count = tok.shape[2]
    feat = tok.shape[3]
    width = wg.shape[1]
    out_width = wd.shape[1]
    slots = range(1, tok.shape[0])

    def peer(slot):
        node = n
        if slot & 1:
            node = node + 1 - 2 * lax.rem(node, 2)
        if slot & 4:
            node = lax.rem(node + group_count // 2, group_count)
        member = lax.rem(l + 1, member_count) if slot & 2 else l
        return {"node": node, "local": member}

    first = pltpu.make_async_copy(tok_in, tok.at[0, c], loc_sem.at[0])
    first.start()
    loads = []
    for index, (src, dst) in enumerate(
        ((sg_in, sg), (su_in, su), (wg_in, wg), (wu_in, wu), (wd_in, wd), (sd_in, sd))
    ):
        loads.append(pltpu.make_async_copy(src, dst, loc_sem.at[2 + index]))

    barrier = pltpu.get_barrier_semaphore()
    for slot in slots:
        pl.semaphore_signal(barrier, inc=1, device_id=peer(slot), device_id_type=MESH)

    @pl.when(c > 0)
    def _():
        pl.semaphore_signal(barrier, inc=1, device_id={"ctx": c - 1}, device_id_type=MESH)

    @pl.when(c < last)
    def _():
        pl.semaphore_signal(barrier, inc=1, device_id={"ctx": c + 1}, device_id_type=MESH)

    for load in loads:
        load.start()

    inner = (c > 0) & (c < last)

    @pl.when(inner)
    def _():
        pl.semaphore_wait(barrier, len(slots) + 2)

    @pl.when(jnp.logical_not(inner))
    def _():
        pl.semaphore_wait(barrier, len(slots) + 1)

    first.wait()

    SHARED = 2
    PAIR = 3
    half_rows = tok_count // 2

    def piece(chunk, shard):
        if chunk < 2:
            return tok.at[0, shard, pl.ds(chunk * half_rows, half_rows)]
        if chunk == SHARED:
            return hid_s.at[shard]
        return hid.at[chunk - PAIR, shard]

    def line(chunk, depth, way, shard, target):
        return pltpu.make_async_remote_copy(
            src_ref=piece(chunk, shard),
            dst_ref=piece(chunk, shard),
            send_sem=z_send.at[way, depth, chunk],
            recv_sem=z_recv.at[way, depth, chunk],
            device_id={"ctx": target},
            device_id_type=MESH,
        )

    def line_send(chunk, depth, finish=False, only=None):
        for way in (0, 1):
            shard, target = (c - depth, c + 1) if way == 0 else (c + depth, c - 1)
            ready = (c >= depth) & (c < last) if way == 0 else (c + depth <= last) & (c > 0)
            if PAIR <= chunk < PAIR + 3 and depth == 0:
                ready = ready & (c != (last - 1 if way == 0 else 1))
            if only is not None:
                ready = ready & only

            @pl.when(ready)
            def _():
                copy = line(chunk, depth, way, shard, target)
                if finish:
                    copy.wait_send()
                else:
                    copy.start()

    def line_take(chunk, depth, relays, then=None):
        for way in (0, 1):
            shard = c - 1 - depth if way == 0 else c + 1 + depth
            source = c - 1 if way == 0 else c + 1
            target = c + 1 if way == 0 else c - 1
            here = shard >= 0 if way == 0 else shard <= last
            passes = target < ctx_count if way == 0 else target >= 0
            if depth == last - 1:
                if relays:
                    continue
            else:
                here = here & (passes if relays else jnp.logical_not(passes))
            if PAIR <= chunk < PAIR + 3 and depth == 0 and not relays:
                continue

            @pl.when(here)
            def _():
                line(chunk, depth, way, shard, source).wait_recv()
                if relays:
                    line(chunk, depth + 1, way, shard, target).start()
                if then is not None:
                    then(shard)

    def await_line(chunk, depths):
        for depth in depths:
            line_take(chunk, depth, False)

    def relay(chunk, kind):
        depth = 1 if kind == "far" else 0
        for way in (0, 1):
            me = 1 if (way == 0) == (kind == "edge") else last - 1
            shard = c - 1 - depth if way == 0 else c + 1 + depth
            source = c - 1 if way == 0 else c + 1
            target = c + 1 if way == 0 else c - 1

            @pl.when(c == me)
            def _():
                line(chunk, depth, way, shard, source).wait_recv()
                line(chunk, depth + 1, way, shard, target).start()

    def at_stage(stage, then):
        if stage == 0:
            then(c)
            return
        for shard in (c - stage, c + stage):

            @pl.when((shard >= 0) & (shard <= last))
            def _():
                then(shard)

    def hand(src_slot, dst_slot, shard, over):
        return pltpu.make_async_remote_copy(
            src_ref=tok.at[src_slot, shard],
            dst_ref=tok.at[dst_slot, shard],
            send_sem=b_send.at[dst_slot, shard],
            recv_sem=b_recv.at[dst_slot, shard],
            device_id=peer(over),
            device_id_type=MESH,
        )

    def spread(shard):
        hand(0, 1, shard, 1).start()
        hand(0, 2, shard, 2).start()
        hand(0, 4, shard, 4).start()

    def take(slot, shard):
        hand(0, slot, shard, 1).wait_recv()

    line_send(0, 0)
    line_send(1, 0)

    ends = ((0, 1), (last, last - 1))
    lent = ((0, 3 * width // 4), (3 * width // 4, width // 4))

    def lend(part_index, end, near):
        return pltpu.make_async_remote_copy(
            src_ref=wd.at[pl.ds(near * width + lent[part_index][0], lent[part_index][1])],
            dst_ref=near_wd.at[pl.ds(*lent[part_index])],
            send_sem=w_send.at[part_index],
            recv_sem=w_recv.at[part_index],
            device_id={"ctx": near},
            device_id_type=MESH,
        )

    def lend_start(part_index):
        for end, near in ends:

            @pl.when(c == end)
            def _():
                lend(part_index, end, near).start()

    scores = scores_in[...]
    scaled = route_scale * scores / jnp.sum(scores, axis=0, keepdims=True)
    gates = scaled.astype(jnp.bfloat16).astype(jnp.float32)
    row = lax.broadcasted_iota(jnp.int32, meta.shape[1:], 0)
    named = jnp.zeros(row.shape, jnp.float32)
    table = jnp.zeros(row.shape, jnp.float32)
    for k in range(ids_in.shape[0]):
        expert = ids_in[k : k + 1, :]
        named = jnp.where(row == expert // member_count, 1.0, named)
        table = table + jnp.where(row == expert + group_count, gates[k : k + 1, :], 0.0)
    square = (tok_count, tok_count)
    before = lax.broadcasted_iota(jnp.int32, square, 0) < lax.broadcasted_iota(jnp.int32, square, 1)
    counts = matmul(named.astype(jnp.bfloat16), jnp.where(before, 1.0, 0.0).astype(jnp.bfloat16))
    meta[0] = jnp.where(row < group_count, jnp.where(named > 0.5, counts, -1.0), table)

    greet = []
    for slot in slots:
        greet.append(
            pltpu.make_async_remote_copy(
                src_ref=meta.at[0],
                dst_ref=meta.at[slot],
                send_sem=m_send.at[slot],
                recv_sem=m_recv.at[slot],
                device_id=peer(slot),
                device_id_type=MESH,
            )
        )
        greet[-1].start()
    spread(c)

    def columns(shard):
        return pl.ds(pl.multiple_of(shard * feat, 128), feat)

    def shared_add(shard, fresh=False):
        ins = columns(shard)

        def visit(start, size):
            cols = pl.ds(start, size)
            g = matmul(tok[0, shard], sg[ins, cols])
            u = matmul(tok[0, shard], su[ins, cols])
            sum_g[:, cols] = g if fresh else sum_g[:, cols] + g
            sum_u[:, cols] = u if fresh else sum_u[:, cols] + u

        column_tiles(width, 256, visit)

    rank_of = lambda slot: meta[slot, pl.ds(n, 1), :]
    weight_of = lambda slot: meta[slot, pl.ds(group_count + n * member_count + l, 1), :]

    def mask_of(slot):
        spots = lax.broadcasted_iota(jnp.int32, (cap, tok_count), 0).astype(jnp.float32)
        return jnp.where(spots == rank_of(slot), 1.0, 0.0).astype(jnp.bfloat16)

    def pair_add(index, shard, fresh=False):
        ins = columns(shard)
        for place, slot in enumerate(pairs[index]):
            chosen = matmul(mask_of(slot), tok[slot, shard]).astype(jnp.bfloat16)
            rows_in[place * cap : (place + 1) * cap, :] = chosen

        def visit(start, size):
            cols = pl.ds(start, size)
            g = matmul(rows_in[...], wg[ins, cols])
            u = matmul(rows_in[...], wu[ins, cols])
            acc_g[index, :, cols] = g if fresh else acc_g[index, :, cols] + g
            acc_u[index, :, cols] = u if fresh else acc_u[index, :, cols] + u

        column_tiles(width, 256, visit)

    def pair_end(index):
        g = acc_g[index]
        hid[index, c] = (g / (1.0 + jnp.exp(-g)) * acc_u[index]).astype(jnp.bfloat16)
        line_send(PAIR + index, 0)

    pairs = ((2, 3), (4, 5), (6, 7), (0, 1))

    half = ctx_count // 2

    loads[0].wait()
    loads[1].wait()
    shared_add(c, True)
    greet[0].wait_recv()
    loads[2].wait()
    loads[3].wait()
    take(1, c)
    pair_add(3, c, True)
    loads[4].wait()
    lend_start(0)

    def both_add(shard):
        shared_add(shard)
        take(1, shard)
        pair_add(3, shard)

    for depth in range(last):
        for chunk, then in ((0, None), (1, spread)):
            for relays in (True, False):
                line_take(chunk, depth, relays, then)
        at_stage(depth + 1, both_add)

    pair_end(3)
    g = sum_g[...]
    hid_s[c] = (g / (1.0 + jnp.exp(-g)) * sum_u[...]).astype(jnp.bfloat16)
    line_send(SHARED, 0, only=inner)
    lend_start(1)

    def pass_on(shard):
        take(2, shard)
        hand(2, 3, shard, 1).start()

        @pl.when(shard < half)
        def _():
            hand(2, 6, shard, 4).start()

        take(4, shard)
        hand(4, 5, shard, 1).start()

        @pl.when(shard >= half)
        def _():
            hand(4, 6, shard, 2).start()

    def absorb(index, stage):
        def add(shard):
            take(pairs[index][1], shard)
            pair_add(index, shard, stage == 0)

        at_stage(stage, add)

    at_stage(0, pass_on)
    at_stage(1, pass_on)
    for copy in greet[1:]:
        copy.wait_recv()
    absorb(0, 0)
    absorb(1, 0)
    relay(PAIR + 3, "near")
    at_stage(2, pass_on)
    at_stage(3, pass_on)
    for stage in range(1, ctx_count):
        absorb(0, stage)
    relay(PAIR + 3, "edge")
    pair_end(0)
    relay(SHARED, "near")
    for stage in range(1, ctx_count):
        absorb(1, stage)
    pair_end(1)

    loads[5].wait()

    def product(index, shards, cols):
        value = None
        for shard in shards:
            units = shard * width
            if not isinstance(shard, int):
                units = pl.multiple_of(units, 128)
            units = pl.ds(units, width)
            term = matmul(hid[index, shard], wd[units, cols])
            value = term if value is None else value + term
        return value

    def shared_out(shard, fresh=False):
        units = pl.ds(pl.multiple_of(shard * width, 128), width)

        def visit(start, size):
            cols = pl.ds(start, size)
            value = matmul(hid_s[shard], sd[units, cols])
            total[:, cols] = value if fresh else total[:, cols] + value

        column_tiles(out_width, 256, visit)

    split = -(-out_width // 256) * 128
    parts = ((0, split), (split, out_width - split))

    def ship(slot, over, part_index):
        cols = pl.ds(*parts[part_index])
        return pltpu.make_async_remote_copy(
            src_ref=part.at[slot - 1, :, cols],
            dst_ref=got.at[slot - 1, :, cols],
            send_sem=p_send.at[slot, part_index],
            recv_sem=p_recv.at[slot, part_index],
            device_id=peer(over),
            device_id_type=MESH,
        )

    def tiles(part_index, visit):
        begin, size = parts[part_index]

        def shifted(start, count):
            at = begin + start
            visit(at if isinstance(at, int) else pl.multiple_of(at, 128), count)

        column_tiles(size, 256, shifted)

    def mix(index, rows, cols, whole, held, outgoing):
        for place, slot in enumerate(pairs[index]):
            value = matmul(blend[slot, :, 0:cap], rows[place * cap : (place + 1) * cap])
            if slot == 0:
                whole(cols, value)
            elif place == 0:
                held[:, cols] = value
            else:
                outgoing[slot - 1, :, cols] = value.astype(jnp.bfloat16)

    def finish(index):
        def add_total(cols, value):
            total[:, cols] += value

        for part_index in range(2):
            if index < 3:
                for shards, where in (
                    ((0, 1, 2, 3), inner),
                    ((c, c + 2, c + 3), c == 0),
                    ((c, c - 2, c - 3), c == last),
                ):

                    @pl.when(where)
                    def _():
                        def visit(start, size):
                            cols = pl.ds(start, size)
                            rows_out[:, cols] = product(index, shards, cols).astype(jnp.bfloat16)

                        tiles(part_index, visit)

            def visit(start, size):
                cols = pl.ds(start, size)
                if index < 3:
                    rows = rows_out[:, cols]
                else:
                    rows = product(index, range(ctx_count), cols).astype(jnp.bfloat16)
                mix(index, rows, cols, add_total, hold, part)

            tiles(part_index, visit)
            ship(pairs[index][1], 1, part_index).start()

    def forward(index):
        slot, other = pairs[index]

        def visit(start, size):
            cols = pl.ds(start, size)
            value = hold[:, cols] + got[other - 1, :, cols].astype(jnp.float32)
            part[slot - 1, :, cols] = value.astype(jnp.bfloat16)

        for part_index in range(2):
            ship(other, 1, part_index).wait_recv()
            tiles(part_index, visit)
            ship(slot, slot, part_index).start()

    def near_ship(slot, over):
        return pltpu.make_async_remote_copy(
            src_ref=near_part.at[slot - 1],
            dst_ref=near_got.at[slot - 1],
            send_sem=x_send.at[slot],
            recv_sem=x_recv.at[slot],
            device_id=peer(over),
            device_id_type=MESH,
        )

    def near_finish(index):
        def visit(start, size):
            cols = pl.ds(start, size)
            rows = matmul(hid[index, c], near_wd[:, cols]).astype(jnp.bfloat16)
            mix(index, rows, cols, None, near_hold.at[index], near_part)

        column_tiles(out_width, 256, visit)
        near_ship(pairs[index][1], 1).start()

    def near_forward(index):
        slot, other = pairs[index]
        near_ship(other, 1).wait_recv()

        def visit(start, size):
            cols = pl.ds(start, size)
            value = near_hold[index, :, cols] + near_got[other - 1, :, cols].astype(jnp.float32)
            near_part[slot - 1, :, cols] = value.astype(jnp.bfloat16)

        column_tiles(out_width, 256, visit)
        near_ship(slot, slot).start()

    def to_end(end):
        return pltpu.make_async_remote_copy(
            src_ref=near_sum,
            dst_ref=end_sum,
            send_sem=x_send.at[0],
            recv_sem=x_recv.at[0],
            device_id={"ctx": end},
            device_id_type=MESH,
        )

    def on_inner(step, *args):
        @pl.when(inner)
        def _():
            step(*args)

    def lent_wait():
        for part_index in range(2):
            lend(part_index, c, c).wait_recv()

    def take_pair(shards):
        for shard in shards:
            take(6, shard)
            hand(6, 7, shard, 1).start()

    def add_pair(shards):
        for shard in shards:
            take(7, shard)
            pair_add(2, shard, shard == 0)

    for slot in range(tok.shape[0]):
        spots = lax.broadcasted_iota(jnp.int32, (tok_count, tok_count), 0).astype(jnp.float32)
        mask = jnp.where(spots == rank_of(slot), weight_of(slot), 0.0)
        blend[slot] = jnp.transpose(mask).astype(jnp.bfloat16)
    relay(PAIR + 3, "far")
    take_pair(range(half))
    add_pair(range(half))
    relay(PAIR, "near")
    relay(PAIR, "edge")
    take_pair(range(half, ctx_count))
    add_pair(range(half, ctx_count - 1))
    relay(PAIR + 1, "near")
    relay(PAIR + 1, "edge")
    add_pair(range(ctx_count - 1, ctx_count))
    pair_end(2)
    line_send(SHARED, 0, only=jnp.logical_not(inner))
    on_inner(lent_wait)
    on_inner(near_finish, 0)
    relay(PAIR, "far")
    on_inner(near_finish, 2)
    relay(PAIR + 2, "edge")
    relay(PAIR + 1, "far")
    on_inner(near_finish, 1)
    on_inner(near_forward, 2)
    on_inner(near_forward, 0)
    on_inner(near_forward, 1)
    relay(PAIR + 2, "near")
    relay(SHARED, "edge")
    relay(PAIR + 2, "far")
    shared_out(c, True)
    await_line(PAIR + 3, range(last))
    finish(3)
    relay(SHARED, "far")
    await_line(PAIR, range(last))
    finish(0)
    forward(0)

    @pl.when(inner)
    def _():
        for slot in (2, 4, 6):
            near_ship(slot, slot).wait_recv()

        def visit(start, size):
            cols = pl.ds(start, size)
            value = near_got[1, :, cols].astype(jnp.float32)
            for slot in (4, 6):
                value = value + near_got[slot - 1, :, cols].astype(jnp.float32)
            near_sum[:, cols] = value.astype(jnp.bfloat16)

        column_tiles(out_width, 256, visit)

    for end, near in ends:

        @pl.when(c == near)
        def _():
            to_end(end).start()

    await_line(PAIR + 1, range(last))
    finish(1)
    forward(1)
    await_line(SHARED, range(last - 1))
    for stage in range(1, last):
        at_stage(stage, shared_out)
    await_line(PAIR + 2, range(last))
    finish(2)
    forward(2)

    def gather_some(start, size):
        cols = pl.ds(start, size)
        value = total[:, cols]
        for slot in (1, 2, 4):
            value = value + got[slot - 1, :, cols].astype(jnp.float32)
        total[:, cols] = value

    for slot in (1, 2, 4):
        for part_index in range(2):
            ship(slot, slot, part_index).wait_recv()
    column_tiles(out_width, 256, gather_some)
    await_line(SHARED, (last - 1,))
    at_stage(last, shared_out)

    @pl.when(jnp.logical_not(inner))
    def _():
        to_end(c).wait_recv()

        def visit(start, size):
            cols = pl.ds(start, size)
            total[:, cols] += end_sum[:, cols].astype(jnp.float32)

        column_tiles(out_width, 256, visit)

    def gather_rest(start, size):
        cols = pl.ds(start, size)
        value = total[:, cols] + got[5, :, cols].astype(jnp.float32)
        out_ref[:, cols] = value.astype(jnp.bfloat16)

    for part_index in range(2):
        ship(6, 6, part_index).wait_recv()
        tiles(part_index, gather_rest)

    for slot in slots:
        for part_index in range(2):
            ship(slot, slot, part_index).wait_send()
    for copy in greet:
        copy.wait_send()

    @pl.when(inner)
    def _():
        for slot in slots[1:]:
            near_ship(slot, slot).wait_send()
        to_end(c).wait_send()

    @pl.when(jnp.logical_not(inner))
    def _():
        for part_index in range(2):
            lend(part_index, c, 1).wait_send()

    for chunk in range(PAIR + 4):
        for depth in range(last):
            line_send(chunk, depth, finish=True)
    for shard in range(ctx_count):
        for slot in (1, 2, 3, 4, 5, 6, 7):
            hand(0, slot, shard, 1).wait_send()


def cube(
    tokens, expert_ids, route_scores, w_gate, w_up, w_down, shared_gate, shared_up, shared_down
):
    ctx_count = lax.axis_size("ctx")
    group_count = lax.axis_size("node")
    member_count = lax.axis_size("local")
    expert_count = group_count * member_count
    tok_count, feat = tokens.shape
    cap = (10 * tok_count + 4 * group_count - 1) // (4 * group_count)
    hidden_units, out_width = w_down.shape[1:]
    width = w_gate.shape[2]
    meta_rows = -(-(group_count + expert_count) // 16) * 16
    slots = 2 * group_count
    bf16 = jnp.bfloat16
    anywhere = pl.BlockSpec(memory_space=pl.ANY)
    inside = pl.BlockSpec(memory_space=pltpu.VMEM)
    dma = pltpu.SemaphoreType.DMA
    kernel = lambda *refs: cube_kernel((ctx_count, group_count, member_count, cap), *refs)
    return pl.pallas_call(
        kernel,
        out_shape=jax.ShapeDtypeStruct((tok_count, out_width), bf16),
        in_specs=[anywhere, inside, inside] + [anywhere] * 6,
        out_specs=inside,
        scratch_shapes=[
            pltpu.VMEM((slots, ctx_count, tok_count, feat), bf16),
            pltpu.VMEM((slots, meta_rows, tok_count), jnp.float32),
            pltpu.VMEM(w_gate.shape[1:], bf16),
            pltpu.VMEM(w_up.shape[1:], bf16),
            pltpu.VMEM(w_down.shape[1:], bf16),
            pltpu.VMEM(shared_gate.shape, bf16),
            pltpu.VMEM(shared_up.shape, bf16),
            pltpu.VMEM(shared_down.shape, bf16),
            pltpu.VMEM((2 * cap, feat), bf16),
            pltpu.VMEM((ctx_count, tok_count, width), bf16),
            pltpu.VMEM((4, ctx_count, 2 * cap, width), bf16),
            pltpu.VMEM((slots - 1, tok_count, out_width), bf16),
            pltpu.VMEM((slots - 1, tok_count, out_width), bf16),
            pltpu.VMEM((tok_count, out_width), jnp.float32),
            pltpu.VMEM((tok_count, width), jnp.float32),
            pltpu.VMEM((tok_count, width), jnp.float32),
            pltpu.VMEM((4, 2 * cap, width), jnp.float32),
            pltpu.VMEM((4, 2 * cap, width), jnp.float32),
            pltpu.VMEM((tok_count, out_width), jnp.float32),
            pltpu.VMEM((slots, tok_count, tok_count), bf16),
            pltpu.VMEM((2 * cap, out_width), bf16),
            pltpu.VMEM((width, out_width), bf16),
            pltpu.VMEM((slots - 1, tok_count, out_width), bf16),
            pltpu.VMEM((slots - 1, tok_count, out_width), bf16),
            pltpu.VMEM((3, tok_count, out_width), jnp.float32),
            pltpu.VMEM((tok_count, out_width), bf16),
            pltpu.VMEM((tok_count, out_width), bf16),
            dma((8,)),
            dma((2, ctx_count - 1, 7)),
            dma((2, ctx_count - 1, 7)),
            dma((slots, ctx_count)),
            dma((slots, ctx_count)),
            dma((slots,)),
            dma((slots,)),
            dma((slots, 2)),
            dma((slots, 2)),
            dma((2,)),
            dma((2,)),
            dma((slots,)),
            dma((slots,)),
        ],
        compiler_params=pltpu.CompilerParams(
            collective_id=0, has_side_effects=True, vmem_limit_bytes=VMEM_BYTES
        ),
    )(
        tokens,
        expert_ids.T,
        route_scores.T,
        w_gate[0],
        w_up[0],
        w_down[0],
        shared_gate,
        shared_up,
        shared_down,
    )


def local(tokens, expert_ids, *rest):
    whole_groups = expert_ids.shape[1] == 2 * lax.axis_size("local")
    sizes = (lax.axis_size("ctx"), lax.axis_size("node"), lax.axis_size("local"))
    if whole_groups and sizes == (4, 4, 2):
        return cube(tokens, expert_ids, *rest)
    return exchange(tokens, expert_ids, *rest)


def solution(mesh):
    return jax.shard_map(
        local,
        mesh=mesh,
        in_specs=(
            P(("node", "local"), "ctx"),
            P(("node", "local"), None),
            P(("node", "local"), None),
            P(("node", "local"), None, "ctx"),
            P(("node", "local"), None, "ctx"),
            P(("node", "local"), None, "ctx"),
            P(None, "ctx"),
            P(None, "ctx"),
            P(None, "ctx"),
        ),
        out_specs=P(("node", "local"), "ctx"),
        check_vma=False,
    )
```

```python
import jax
import jax.numpy as jnp
from jax import lax
from jax.experimental import pallas as pl
from jax.experimental.pallas import tpu as pltpu
from jax.sharding import PartitionSpec as P

route_scale = 2.5
MESH = pl.DeviceIdType.MESH
VMEM_BYTES = 64000 * 1024


def matmul(left_side, right_side):
    return jnp.dot(left_side, right_side, preferred_element_type=jnp.float32)


def exchange(
    tokens, expert_ids, route_scores, w_gate, w_up, w_down, shared_gate, shared_up, shared_down
):
    tok_count = tokens.shape[0]
    feat_local = tokens.shape[1]
    top_count = expert_ids.shape[1]
    group_count = lax.axis_size("node")
    member_count = lax.axis_size("local")
    expert_count = group_count * member_count
    group_cap = (10 * tok_count + 4 * group_count - 1) // (4 * group_count)
    capacity = (2 * group_cap + member_count - 1) // member_count
    slot_total = expert_count * capacity
    gate_local = w_gate[0]
    up_local = w_up[0]
    down_local = w_down[0]
    out_width = down_local.shape[1]
    scaled = route_scale * route_scores / jnp.sum(route_scores, axis=1, keepdims=True)
    gate_weights = lax.optimization_barrier(scaled.astype(jnp.bfloat16)).astype(jnp.float32)
    group_range = jnp.arange(group_count, dtype=jnp.int32)
    group_onehot = (expert_ids // member_count)[:, :, None] == group_range[None, None, :]
    flat_ids = expert_ids.reshape(-1)
    pair_count = flat_ids.shape[0]
    onehot = (flat_ids[:, None] == jnp.arange(expert_count, dtype=jnp.int32)[None, :]).astype(
        jnp.int32
    )
    earlier = jnp.cumsum(onehot, axis=0) - onehot
    ranking = jnp.sum(earlier * onehot, axis=1)
    pair_slot = flat_ids * capacity + ranking
    pair_token = jnp.arange(pair_count, dtype=jnp.int32) // top_count
    matches = pair_slot[None, :] == jnp.arange(slot_total, dtype=jnp.int32)[:, None]
    slot_token = jnp.where(
        jnp.any(matches, axis=1),
        jnp.sum(jnp.where(matches, pair_token[None, :], 0), axis=1),
        tok_count,
    )
    padded_tokens = jnp.concatenate([tokens, jnp.zeros((1, feat_local), tokens.dtype)], axis=0)
    send_rows = padded_tokens[slot_token].reshape(group_count, member_count, capacity * feat_local)
    arrived = lax.all_to_all(
        lax.all_to_all(send_rows, "node", split_axis=0, concat_axis=0, tiled=True),
        "local",
        split_axis=1,
        concat_axis=1,
        tiled=True,
    )
    routed_rows = arrived.reshape(slot_total, feat_local)
    stacked = jnp.concatenate([routed_rows, tokens], axis=0)
    segment = lax.all_gather(stacked, "ctx", axis=1, tiled=True)
    routed_part = segment[:slot_total]
    shared_part = segment[slot_total:]
    gate_routed = matmul(routed_part, gate_local)
    up_routed = matmul(routed_part, up_local)
    gate_shared = matmul(shared_part, shared_gate)
    up_shared = matmul(shared_part, shared_up)
    routed_hidden = (jax.nn.silu(gate_routed) * up_routed).astype(jnp.bfloat16)
    shared_hidden = (jax.nn.silu(gate_shared) * up_shared).astype(jnp.bfloat16)
    hidden_stack = jnp.concatenate([routed_hidden, shared_hidden], axis=0)
    segment = lax.all_gather(hidden_stack, "ctx", axis=1, tiled=True)
    routed_out = matmul(segment[:slot_total], down_local)
    shared_out = matmul(segment[slot_total:], shared_down)
    routed_bf = routed_out.astype(jnp.bfloat16)
    sendback = routed_bf.reshape(group_count, member_count, capacity * out_width)
    returned = lax.all_to_all(
        lax.all_to_all(sendback, "node", split_axis=0, concat_axis=0, tiled=True),
        "local",
        split_axis=1,
        concat_axis=1,
        tiled=True,
    )
    returned = returned.reshape(slot_total, out_width)
    pair_out = returned[pair_slot].reshape(tok_count, top_count, out_width).astype(jnp.float32)
    weighted = gate_weights[:, :, None] * pair_out
    group_sum = jnp.einsum(
        "tkg,tkd->tgd", group_onehot.astype(jnp.float32), weighted, precision=lax.Precision.HIGHEST
    )
    rounded = lax.optimization_barrier(group_sum.astype(jnp.bfloat16)).astype(jnp.float32)
    routed_sum = jnp.sum(rounded, axis=1)
    mixed = shared_out + routed_sum
    return mixed.astype(jnp.bfloat16)


def column_tiles(width, tile, visit):
    whole = width // tile
    if whole == 1:
        visit(0, tile)
    elif whole > 1:

        def step(index, carry):
            visit(pl.multiple_of(index * tile, tile), tile)
            return carry

        lax.fori_loop(0, whole, step, 0)
    if width % tile:
        visit(whole * tile, width % tile)


def cube_kernel(
    sizes,
    tok_in,
    ids_in,
    scores_in,
    wg_in,
    wu_in,
    wd_in,
    sg_in,
    su_in,
    sd_in,
    out_ref,
    tok,
    meta,
    wg,
    wu,
    wd,
    sg,
    su,
    sd,
    rows_in,
    hid_s,
    hid,
    part,
    got,
    total,
    sum_g,
    sum_u,
    acc_g,
    acc_u,
    hold,
    blend,
    rows_out,
    near_wd,
    near_part,
    near_got,
    near_hold,
    near_sum,
    end_sum,
    loc_sem,
    z_send,
    z_recv,
    b_send,
    b_recv,
    m_send,
    m_recv,
    p_send,
    p_recv,
    w_send,
    w_recv,
    x_send,
    x_recv,
):
    ctx_count, group_count, member_count, cap = sizes
    c = lax.axis_index("ctx")
    n = lax.axis_index("node")
    l = lax.axis_index("local")
    last = ctx_count - 1
    tok_count = tok.shape[2]
    feat = tok.shape[3]
    width = wg.shape[1]
    out_width = wd.shape[1]
    slots = range(1, tok.shape[0])

    def peer(slot):
        node = n
        if slot & 1:
            node = node + 1 - 2 * lax.rem(node, 2)
        if slot & 4:
            node = lax.rem(node + group_count // 2, group_count)
        member = lax.rem(l + 1, member_count) if slot & 2 else l
        return {"node": node, "local": member}

    first = pltpu.make_async_copy(tok_in, tok.at[0, c], loc_sem.at[0])
    first.start()
    loads = []
    for index, (src, dst) in enumerate(
        ((sg_in, sg), (su_in, su), (wg_in, wg), (wu_in, wu), (wd_in, wd), (sd_in, sd))
    ):
        loads.append(pltpu.make_async_copy(src, dst, loc_sem.at[2 + index]))

    barrier = pltpu.get_barrier_semaphore()
    for slot in slots:
        pl.semaphore_signal(barrier, inc=1, device_id=peer(slot), device_id_type=MESH)

    @pl.when(c > 0)
    def _():
        pl.semaphore_signal(barrier, inc=1, device_id={"ctx": c - 1}, device_id_type=MESH)

    @pl.when(c < last)
    def _():
        pl.semaphore_signal(barrier, inc=1, device_id={"ctx": c + 1}, device_id_type=MESH)

    for load in loads:
        load.start()

    inner = (c > 0) & (c < last)

    @pl.when(inner)
    def _():
        pl.semaphore_wait(barrier, len(slots) + 2)

    @pl.when(jnp.logical_not(inner))
    def _():
        pl.semaphore_wait(barrier, len(slots) + 1)

    first.wait()

    SHARED = 2
    PAIR = 3
    half_rows = tok_count // 2

    def piece(chunk, shard):
        if chunk < 2:
            return tok.at[0, shard, pl.ds(chunk * half_rows, half_rows)]
        if chunk == SHARED:
            return hid_s.at[shard]
        return hid.at[chunk - PAIR, shard]

    def line(chunk, depth, way, shard, target):
        return pltpu.make_async_remote_copy(
            src_ref=piece(chunk, shard),
            dst_ref=piece(chunk, shard),
            send_sem=z_send.at[way, depth, chunk],
            recv_sem=z_recv.at[way, depth, chunk],
            device_id={"ctx": target},
            device_id_type=MESH,
        )

    def line_send(chunk, depth, finish=False, only=None):
        for way in (0, 1):
            shard, target = (c - depth, c + 1) if way == 0 else (c + depth, c - 1)
            ready = (c >= depth) & (c < last) if way == 0 else (c + depth <= last) & (c > 0)
            if PAIR <= chunk < PAIR + 3 and depth == 0:
                ready = ready & (c != (last - 1 if way == 0 else 1))
            if only is not None:
                ready = ready & only

            @pl.when(ready)
            def _():
                copy = line(chunk, depth, way, shard, target)
                if finish:
                    copy.wait_send()
                else:
                    copy.start()

    def line_take(chunk, depth, relays, then=None):
        for way in (0, 1):
            shard = c - 1 - depth if way == 0 else c + 1 + depth
            source = c - 1 if way == 0 else c + 1
            target = c + 1 if way == 0 else c - 1
            here = shard >= 0 if way == 0 else shard <= last
            passes = target < ctx_count if way == 0 else target >= 0
            if depth == last - 1:
                if relays:
                    continue
            else:
                here = here & (passes if relays else jnp.logical_not(passes))
            if PAIR <= chunk < PAIR + 3 and depth == 0 and not relays:
                continue

            @pl.when(here)
            def _():
                line(chunk, depth, way, shard, source).wait_recv()
                if relays:
                    line(chunk, depth + 1, way, shard, target).start()
                if then is not None:
                    then(shard)

    def await_line(chunk, depths):
        for depth in depths:
            line_take(chunk, depth, False)

    def relay(chunk, kind):
        depth = 1 if kind == "far" else 0
        for way in (0, 1):
            me = 1 if (way == 0) == (kind == "edge") else last - 1
            shard = c - 1 - depth if way == 0 else c + 1 + depth
            source = c - 1 if way == 0 else c + 1
            target = c + 1 if way == 0 else c - 1

            @pl.when(c == me)
            def _():
                line(chunk, depth, way, shard, source).wait_recv()
                line(chunk, depth + 1, way, shard, target).start()

    def at_stage(stage, then):
        if stage == 0:
            then(c)
            return
        for shard in (c - stage, c + stage):

            @pl.when((shard >= 0) & (shard <= last))
            def _():
                then(shard)

    def hand(src_slot, dst_slot, shard, over):
        return pltpu.make_async_remote_copy(
            src_ref=tok.at[src_slot, shard],
            dst_ref=tok.at[dst_slot, shard],
            send_sem=b_send.at[dst_slot, shard],
            recv_sem=b_recv.at[dst_slot, shard],
            device_id=peer(over),
            device_id_type=MESH,
        )

    def spread(shard):
        hand(0, 1, shard, 1).start()
        hand(0, 2, shard, 2).start()
        hand(0, 4, shard, 4).start()

    def take(slot, shard):
        hand(0, slot, shard, 1).wait_recv()

    line_send(0, 0)
    line_send(1, 0)

    ends = ((0, 1), (last, last - 1))
    lent = ((0, 3 * width // 4), (3 * width // 4, width // 4))

    def lend(part_index, end, near):
        return pltpu.make_async_remote_copy(
            src_ref=wd.at[pl.ds(near * width + lent[part_index][0], lent[part_index][1])],
            dst_ref=near_wd.at[pl.ds(*lent[part_index])],
            send_sem=w_send.at[part_index],
            recv_sem=w_recv.at[part_index],
            device_id={"ctx": near},
            device_id_type=MESH,
        )

    def lend_start(part_index):
        for end, near in ends:

            @pl.when(c == end)
            def _():
                lend(part_index, end, near).start()

    scores = scores_in[...]
    scaled = route_scale * scores / jnp.sum(scores, axis=0, keepdims=True)
    gates = scaled.astype(jnp.bfloat16).astype(jnp.float32)
    row = lax.broadcasted_iota(jnp.int32, meta.shape[1:], 0)
    named = jnp.zeros(row.shape, jnp.float32)
    table = jnp.zeros(row.shape, jnp.float32)
    for k in range(ids_in.shape[0]):
        expert = ids_in[k : k + 1, :]
        named = jnp.where(row == expert // member_count, 1.0, named)
        table = table + jnp.where(row == expert + group_count, gates[k : k + 1, :], 0.0)
    square = (tok_count, tok_count)
    before = lax.broadcasted_iota(jnp.int32, square, 0) < lax.broadcasted_iota(jnp.int32, square, 1)
    counts = matmul(named.astype(jnp.bfloat16), jnp.where(before, 1.0, 0.0).astype(jnp.bfloat16))
    meta[0] = jnp.where(row < group_count, jnp.where(named > 0.5, counts, -1.0), table)

    greet = []
    for slot in slots:
        greet.append(
            pltpu.make_async_remote_copy(
                src_ref=meta.at[0],
                dst_ref=meta.at[slot],
                send_sem=m_send.at[slot],
                recv_sem=m_recv.at[slot],
                device_id=peer(slot),
                device_id_type=MESH,
            )
        )
        greet[-1].start()
    spread(c)

    def columns(shard):
        return pl.ds(pl.multiple_of(shard * feat, 128), feat)

    def shared_add(shard, fresh=False):
        ins = columns(shard)

        def visit(start, size):
            cols = pl.ds(start, size)
            g = matmul(tok[0, shard], sg[ins, cols])
            u = matmul(tok[0, shard], su[ins, cols])
            sum_g[:, cols] = g if fresh else sum_g[:, cols] + g
            sum_u[:, cols] = u if fresh else sum_u[:, cols] + u

        column_tiles(width, 256, visit)

    rank_of = lambda slot: meta[slot, pl.ds(n, 1), :]
    weight_of = lambda slot: meta[slot, pl.ds(group_count + n * member_count + l, 1), :]

    def mask_of(slot):
        spots = lax.broadcasted_iota(jnp.int32, (cap, tok_count), 0).astype(jnp.float32)
        return jnp.where(spots == rank_of(slot), 1.0, 0.0).astype(jnp.bfloat16)

    def pair_add(index, shard, fresh=False):
        ins = columns(shard)
        for place, slot in enumerate(pairs[index]):
            chosen = matmul(mask_of(slot), tok[slot, shard]).astype(jnp.bfloat16)
            rows_in[place * cap : (place + 1) * cap, :] = chosen

        def visit(start, size):
            cols = pl.ds(start, size)
            g = matmul(rows_in[...], wg[ins, cols])
            u = matmul(rows_in[...], wu[ins, cols])
            acc_g[index, :, cols] = g if fresh else acc_g[index, :, cols] + g
            acc_u[index, :, cols] = u if fresh else acc_u[index, :, cols] + u

        column_tiles(width, 256, visit)

    def pair_end(index):
        g = acc_g[index]
        hid[index, c] = (g / (1.0 + jnp.exp(-g)) * acc_u[index]).astype(jnp.bfloat16)
        line_send(PAIR + index, 0)

    pairs = ((2, 3), (4, 5), (6, 7), (0, 1))

    half = ctx_count // 2

    loads[0].wait()
    loads[1].wait()
    shared_add(c, True)
    greet[0].wait_recv()
    loads[2].wait()
    loads[3].wait()
    take(1, c)
    pair_add(3, c, True)
    loads[4].wait()
    lend_start(0)

    def both_add(shard):
        shared_add(shard)
        take(1, shard)
        pair_add(3, shard)

    for depth in range(last):
        for chunk, then in ((0, None), (1, spread)):
            for relays in (True, False):
                line_take(chunk, depth, relays, then)
        at_stage(depth + 1, both_add)

    pair_end(3)
    g = sum_g[...]
    hid_s[c] = (g / (1.0 + jnp.exp(-g)) * sum_u[...]).astype(jnp.bfloat16)
    line_send(SHARED, 0, only=inner)
    lend_start(1)

    def pass_on(shard):
        take(2, shard)
        hand(2, 3, shard, 1).start()

        @pl.when(shard < half)
        def _():
            hand(2, 6, shard, 4).start()

        take(4, shard)
        hand(4, 5, shard, 1).start()

        @pl.when(shard >= half)
        def _():
            hand(4, 6, shard, 2).start()

    def absorb(index, stage):
        def add(shard):
            take(pairs[index][1], shard)
            pair_add(index, shard, stage == 0)

        at_stage(stage, add)

    at_stage(0, pass_on)
    at_stage(1, pass_on)
    for copy in greet[1:]:
        copy.wait_recv()
    absorb(0, 0)
    absorb(1, 0)
    relay(PAIR + 3, "near")
    at_stage(2, pass_on)
    at_stage(3, pass_on)
    for stage in range(1, ctx_count):
        absorb(0, stage)
    relay(PAIR + 3, "edge")
    pair_end(0)
    relay(SHARED, "near")
    for stage in range(1, ctx_count):
        absorb(1, stage)
    pair_end(1)

    loads[5].wait()

    def product(index, shards, cols):
        value = None
        for shard in shards:
            units = shard * width
            if not isinstance(shard, int):
                units = pl.multiple_of(units, 128)
            units = pl.ds(units, width)
            term = matmul(hid[index, shard], wd[units, cols])
            value = term if value is None else value + term
        return value

    def shared_out(shard, fresh=False):
        units = pl.ds(pl.multiple_of(shard * width, 128), width)

        def visit(start, size):
            cols = pl.ds(start, size)
            value = matmul(hid_s[shard], sd[units, cols])
            total[:, cols] = value if fresh else total[:, cols] + value

        column_tiles(out_width, 256, visit)

    split = -(-out_width // 256) * 128
    parts = ((0, split), (split, out_width - split))

    def ship(slot, over, part_index):
        cols = pl.ds(*parts[part_index])
        return pltpu.make_async_remote_copy(
            src_ref=part.at[slot - 1, :, cols],
            dst_ref=got.at[slot - 1, :, cols],
            send_sem=p_send.at[slot, part_index],
            recv_sem=p_recv.at[slot, part_index],
            device_id=peer(over),
            device_id_type=MESH,
        )

    def tiles(part_index, visit):
        begin, size = parts[part_index]

        def shifted(start, count):
            at = begin + start
            visit(at if isinstance(at, int) else pl.multiple_of(at, 128), count)

        column_tiles(size, 256, shifted)

    def mix(index, rows, cols, whole, held, outgoing):
        for place, slot in enumerate(pairs[index]):
            value = matmul(blend[slot, :, 0:cap], rows[place * cap : (place + 1) * cap])
            if slot == 0:
                whole(cols, value)
            elif place == 0:
                held[:, cols] = value
            else:
                outgoing[slot - 1, :, cols] = value.astype(jnp.bfloat16)

    def finish(index):
        def add_total(cols, value):
            total[:, cols] += value

        for part_index in range(2):
            if index < 3:
                for shards, where in (
                    ((0, 1, 2, 3), inner),
                    ((c, c + 2, c + 3), c == 0),
                    ((c, c - 2, c - 3), c == last),
                ):

                    @pl.when(where)
                    def _():
                        def visit(start, size):
                            cols = pl.ds(start, size)
                            rows_out[:, cols] = product(index, shards, cols).astype(jnp.bfloat16)

                        tiles(part_index, visit)

            def visit(start, size):
                cols = pl.ds(start, size)
                if index < 3:
                    rows = rows_out[:, cols]
                else:
                    rows = product(index, range(ctx_count), cols).astype(jnp.bfloat16)
                mix(index, rows, cols, add_total, hold, part)

            tiles(part_index, visit)
            ship(pairs[index][1], 1, part_index).start()

    def forward(index):
        slot, other = pairs[index]

        def visit(start, size):
            cols = pl.ds(start, size)
            value = hold[:, cols] + got[other - 1, :, cols].astype(jnp.float32)
            part[slot - 1, :, cols] = value.astype(jnp.bfloat16)

        for part_index in range(2):
            ship(other, 1, part_index).wait_recv()
            tiles(part_index, visit)
            ship(slot, slot, part_index).start()

    def near_ship(slot, over):
        return pltpu.make_async_remote_copy(
            src_ref=near_part.at[slot - 1],
            dst_ref=near_got.at[slot - 1],
            send_sem=x_send.at[slot],
            recv_sem=x_recv.at[slot],
            device_id=peer(over),
            device_id_type=MESH,
        )

    def near_finish(index):
        def visit(start, size):
            cols = pl.ds(start, size)
            rows = matmul(hid[index, c], near_wd[:, cols]).astype(jnp.bfloat16)
            mix(index, rows, cols, None, near_hold.at[index], near_part)

        column_tiles(out_width, 256, visit)
        near_ship(pairs[index][1], 1).start()

    def near_forward(index):
        slot, other = pairs[index]
        near_ship(other, 1).wait_recv()

        def visit(start, size):
            cols = pl.ds(start, size)
            value = near_hold[index, :, cols] + near_got[other - 1, :, cols].astype(jnp.float32)
            near_part[slot - 1, :, cols] = value.astype(jnp.bfloat16)

        column_tiles(out_width, 256, visit)
        near_ship(slot, slot).start()

    def to_end(end):
        return pltpu.make_async_remote_copy(
            src_ref=near_sum,
            dst_ref=end_sum,
            send_sem=x_send.at[0],
            recv_sem=x_recv.at[0],
            device_id={"ctx": end},
            device_id_type=MESH,
        )

    def on_inner(step, *args):
        @pl.when(inner)
        def _():
            step(*args)

    def lent_wait():
        for part_index in range(2):
            lend(part_index, c, c).wait_recv()

    def take_pair(shards):
        for shard in shards:
            take(6, shard)
            hand(6, 7, shard, 1).start()

    def add_pair(shards):
        for shard in shards:
            take(7, shard)
            pair_add(2, shard, shard == 0)

    for slot in range(tok.shape[0]):
        spots = lax.broadcasted_iota(jnp.int32, (tok_count, tok_count), 0).astype(jnp.float32)
        mask = jnp.where(spots == rank_of(slot), weight_of(slot), 0.0)
        blend[slot] = jnp.transpose(mask).astype(jnp.bfloat16)
    relay(PAIR + 3, "far")
    take_pair(range(half))
    add_pair(range(half))
    relay(PAIR, "near")
    relay(PAIR, "edge")
    take_pair(range(half, ctx_count))
    add_pair(range(half, ctx_count - 1))
    relay(PAIR + 1, "near")
    relay(PAIR + 1, "edge")
    add_pair(range(ctx_count - 1, ctx_count))
    pair_end(2)
    line_send(SHARED, 0, only=jnp.logical_not(inner))
    on_inner(lent_wait)
    on_inner(near_finish, 0)
    relay(PAIR, "far")
    on_inner(near_finish, 2)
    relay(PAIR + 2, "edge")
    relay(PAIR + 1, "far")
    on_inner(near_finish, 1)
    on_inner(near_forward, 2)
    on_inner(near_forward, 0)
    on_inner(near_forward, 1)
    relay(PAIR + 2, "near")
    relay(SHARED, "edge")
    relay(PAIR + 2, "far")
    await_line(PAIR + 3, range(last))

    def own_part():
        shared_out(c, True)
        finish(3)

    def shared_part():
        for stage in range(1, last):
            at_stage(stage, shared_out)

    outer = jnp.logical_not(inner)

    @pl.when(outer)
    def _():
        own_part()

    await_line(PAIR, range(last))
    finish(0)
    forward(0)
    relay(SHARED, "far")

    @pl.when(inner)
    def _():
        for slot in (2, 4, 6):
            near_ship(slot, slot).wait_recv()

        def visit(start, size):
            cols = pl.ds(start, size)
            value = near_got[1, :, cols].astype(jnp.float32)
            for slot in (4, 6):
                value = value + near_got[slot - 1, :, cols].astype(jnp.float32)
            near_sum[:, cols] = value.astype(jnp.bfloat16)

        column_tiles(out_width, 256, visit)

    for end, near in ends:

        @pl.when(c == near)
        def _():
            to_end(end).start()

    await_line(PAIR + 1, range(last))
    finish(1)
    forward(1)
    await_line(SHARED, range(last - 1))

    @pl.when(outer)
    def _():
        shared_part()

    await_line(PAIR + 2, range(last))
    finish(2)
    forward(2)

    @pl.when(inner)
    def _():
        own_part()
        shared_part()

    def gather_some(start, size):
        cols = pl.ds(start, size)
        value = total[:, cols]
        for slot in (1, 2, 4):
            value = value + got[slot - 1, :, cols].astype(jnp.float32)
        total[:, cols] = value

    for slot in (1, 2, 4):
        for part_index in range(2):
            ship(slot, slot, part_index).wait_recv()
    column_tiles(out_width, 256, gather_some)
    await_line(SHARED, (last - 1,))
    at_stage(last, shared_out)

    @pl.when(jnp.logical_not(inner))
    def _():
        to_end(c).wait_recv()

        def visit(start, size):
            cols = pl.ds(start, size)
            total[:, cols] += end_sum[:, cols].astype(jnp.float32)

        column_tiles(out_width, 256, visit)

    def gather_rest(start, size):
        cols = pl.ds(start, size)
        value = total[:, cols] + got[5, :, cols].astype(jnp.float32)
        out_ref[:, cols] = value.astype(jnp.bfloat16)

    for part_index in range(2):
        ship(6, 6, part_index).wait_recv()
        tiles(part_index, gather_rest)

    for slot in slots:
        for part_index in range(2):
            ship(slot, slot, part_index).wait_send()
    for copy in greet:
        copy.wait_send()

    @pl.when(inner)
    def _():
        for slot in slots[1:]:
            near_ship(slot, slot).wait_send()
        to_end(c).wait_send()

    @pl.when(jnp.logical_not(inner))
    def _():
        for part_index in range(2):
            lend(part_index, c, 1).wait_send()

    for chunk in range(PAIR + 4):
        for depth in range(last):
            line_send(chunk, depth, finish=True)
    for shard in range(ctx_count):
        for slot in (1, 2, 3, 4, 5, 6, 7):
            hand(0, slot, shard, 1).wait_send()


def cube(
    tokens, expert_ids, route_scores, w_gate, w_up, w_down, shared_gate, shared_up, shared_down
):
    ctx_count = lax.axis_size("ctx")
    group_count = lax.axis_size("node")
    member_count = lax.axis_size("local")
    expert_count = group_count * member_count
    tok_count, feat = tokens.shape
    cap = (10 * tok_count + 4 * group_count - 1) // (4 * group_count)
    hidden_units, out_width = w_down.shape[1:]
    width = w_gate.shape[2]
    meta_rows = -(-(group_count + expert_count) // 16) * 16
    slots = 2 * group_count
    bf16 = jnp.bfloat16
    anywhere = pl.BlockSpec(memory_space=pl.ANY)
    inside = pl.BlockSpec(memory_space=pltpu.VMEM)
    dma = pltpu.SemaphoreType.DMA
    kernel = lambda *refs: cube_kernel((ctx_count, group_count, member_count, cap), *refs)
    return pl.pallas_call(
        kernel,
        out_shape=jax.ShapeDtypeStruct((tok_count, out_width), bf16),
        in_specs=[anywhere, inside, inside] + [anywhere] * 6,
        out_specs=inside,
        scratch_shapes=[
            pltpu.VMEM((slots, ctx_count, tok_count, feat), bf16),
            pltpu.VMEM((slots, meta_rows, tok_count), jnp.float32),
            pltpu.VMEM(w_gate.shape[1:], bf16),
            pltpu.VMEM(w_up.shape[1:], bf16),
            pltpu.VMEM(w_down.shape[1:], bf16),
            pltpu.VMEM(shared_gate.shape, bf16),
            pltpu.VMEM(shared_up.shape, bf16),
            pltpu.VMEM(shared_down.shape, bf16),
            pltpu.VMEM((2 * cap, feat), bf16),
            pltpu.VMEM((ctx_count, tok_count, width), bf16),
            pltpu.VMEM((4, ctx_count, 2 * cap, width), bf16),
            pltpu.VMEM((slots - 1, tok_count, out_width), bf16),
            pltpu.VMEM((slots - 1, tok_count, out_width), bf16),
            pltpu.VMEM((tok_count, out_width), jnp.float32),
            pltpu.VMEM((tok_count, width), jnp.float32),
            pltpu.VMEM((tok_count, width), jnp.float32),
            pltpu.VMEM((4, 2 * cap, width), jnp.float32),
            pltpu.VMEM((4, 2 * cap, width), jnp.float32),
            pltpu.VMEM((tok_count, out_width), jnp.float32),
            pltpu.VMEM((slots, tok_count, tok_count), bf16),
            pltpu.VMEM((2 * cap, out_width), bf16),
            pltpu.VMEM((width, out_width), bf16),
            pltpu.VMEM((slots - 1, tok_count, out_width), bf16),
            pltpu.VMEM((slots - 1, tok_count, out_width), bf16),
            pltpu.VMEM((3, tok_count, out_width), jnp.float32),
            pltpu.VMEM((tok_count, out_width), bf16),
            pltpu.VMEM((tok_count, out_width), bf16),
            dma((8,)),
            dma((2, ctx_count - 1, 7)),
            dma((2, ctx_count - 1, 7)),
            dma((slots, ctx_count)),
            dma((slots, ctx_count)),
            dma((slots,)),
            dma((slots,)),
            dma((slots, 2)),
            dma((slots, 2)),
            dma((2,)),
            dma((2,)),
            dma((slots,)),
            dma((slots,)),
        ],
        compiler_params=pltpu.CompilerParams(
            collective_id=0, has_side_effects=True, vmem_limit_bytes=VMEM_BYTES
        ),
    )(
        tokens,
        expert_ids.T,
        route_scores.T,
        w_gate[0],
        w_up[0],
        w_down[0],
        shared_gate,
        shared_up,
        shared_down,
    )


def local(tokens, expert_ids, *rest):
    whole_groups = expert_ids.shape[1] == 2 * lax.axis_size("local")
    sizes = (lax.axis_size("ctx"), lax.axis_size("node"), lax.axis_size("local"))
    if whole_groups and sizes == (4, 4, 2):
        return cube(tokens, expert_ids, *rest)
    return exchange(tokens, expert_ids, *rest)


def solution(mesh):
    return jax.shard_map(
        local,
        mesh=mesh,
        in_specs=(
            P(("node", "local"), "ctx"),
            P(("node", "local"), None),
            P(("node", "local"), None),
            P(("node", "local"), None, "ctx"),
            P(("node", "local"), None, "ctx"),
            P(("node", "local"), None, "ctx"),
            P(None, "ctx"),
            P(None, "ctx"),
            P(None, "ctx"),
        ),
        out_specs=P(("node", "local"), "ctx"),
        check_vma=False,
    )
```
